32 devices in a mesh: groups: 2 (over x), gx: 8 (over z, y), gy: 2 (over core).
Axes of the slice: x: 2, y: 2, z: 4, core: 2. Of those that a mesh axis runs over, the one named last changes fastest.
Arguments:
- tokens: bfloat16 [64, 16384], P('groups', 'gx'), parts along dimension 0, may hold values from -6 to 6
- w_query: bfloat16 [16384, 8192], P('gx', 'gy'), may hold values from -0.046875 to 0.046875
- w_key: bfloat16 [16384, 512], P('gx', 'gy'), may hold values from -0.046875 to 0.046875
- w_value: bfloat16 [16384, 512], P('gx', 'gy'), may hold values from -0.046875 to 0.046875
- w_out: bfloat16 [8192, 16384], P('gy', 'gx'), may hold values from -0.0625 to 0.0625
- key_cache: bfloat16 [64, 4, 1024, 128], P(('groups', 'gx'), 'gy'), parts along dimension 0, may hold values from -600 to 600
- value_cache: bfloat16 [64, 4, 1024, 128], P(('groups', 'gx'), 'gy'), parts along dimension 0, may hold values from -6 to 6
- lengths: int32 [64], P(('groups', 'gx')), parts along dimension 0, may hold values from 2 to 1024, as said below
Outputs:
- attended: bfloat16 [64, 16384], P(('groups', 'gy'), 'gx'), parts along dimension 0
The draws below stay inside these ranges and needn't reach their ends.
There are 2 independent parts, one for each index of `groups`. The reference program is written for one: setup_inputs(seed, part) draws one part's arguments, and reference() takes and returns one part's arrays. A program takes and returns all parts, laid end to end along the dimension named above; an argument that names none is the same for every part. Nothing has to cross between parts.
Inputs may be any that keep to these rules, and one draw needn't show every extreme that they name: `lengths`: every row has 2 or more filled slots; some row has all 1024 slots filled.
All inputs are finite; a program needn't handle non-finite values.
Results may differ from the reference program's by a relative error of at most 0.011.
Values may be sent and summed in bfloat16 or wider, within the bound.
A program may use at most 128 MiB of HBM per device.

```python
import jax
import jax.numpy as jnp
from jax import lax

D = 16384
HQ = 64
KVH = 4
HD = 128
CACHE = 1024
BATCH = 32


def draw_key_cache(key, part):
    base = jax.random.normal(key, (BATCH, KVH, CACHE, HD), jnp.float32)
    base = jnp.clip(base, -5.0, 5.0)
    return jnp.clip(base, -600.0, 600.0).astype(jnp.bfloat16)


def draw_lengths(key, part):
    sampled = jax.random.randint(key, (BATCH,), 2, CACHE + 1, dtype=jnp.int32)
    longest = jax.random.randint(jax.random.fold_in(key, 7), (), 0, BATCH, dtype=jnp.int32)
    return sampled.at[longest].set(CACHE)


def level_of(stream_key, shape, cuts, low, high):
    gain = 1.0
    for dim, blocks in cuts:
        heights = jax.random.uniform(jax.random.fold_in(jax.random.fold_in(stream_key, 6), dim), (blocks,), jnp.float32, low / len(cuts), high / len(cuts))
        gain = gain * jnp.repeat(jnp.exp(heights), shape[dim] // blocks).reshape((-1,) + (1,) * (len(shape) - 1 - dim))
    return gain


def noise(key, dims, spread, most, pieces=(), held_as=jnp.bfloat16):
    entries = jax.random.normal(key, dims, jnp.float32) * spread
    if len(pieces) > 0:
        entries = level_of(key, dims, pieces, -0.22, 0.18) * entries
    return jnp.clip(entries, min=-most, max=most).astype(held_as)


def setup_inputs(seed: int = 0, part: int = 0) -> dict:
    streams_of = jax.random.split(jax.random.key(seed), 9)
    part_keys = jax.random.split(jax.random.fold_in(streams_of[8], part), 9)
    return {
        "tokens": noise(part_keys[0], (BATCH, D), 1.0, 6.0, ((1, 8),)),
        "w_query": noise(streams_of[1], (D, HQ * HD), D ** -0.5, 0.046875, ((0, 8), (1, 2))),
        "w_key": noise(streams_of[2], (D, KVH * HD), D ** -0.5, 0.046875, ((0, 8), (1, 2))),
        "w_value": noise(streams_of[3], (D, KVH * HD), D ** -0.5, 0.046875, ((0, 8), (1, 2))),
        "w_out": noise(streams_of[4], (HQ * HD, D), (HQ * HD) ** -0.5, 0.0625, ((0, 2), (1, 8))),
        "key_cache": draw_key_cache(jax.random.fold_in(jax.random.fold_in(streams_of[8], part), 71), part),
        "value_cache": noise(part_keys[6], (BATCH, KVH, CACHE, HD), 1.0, 6.0, ((0, 8), (1, 2))),
        "lengths": draw_lengths(jax.random.fold_in(jax.random.fold_in(streams_of[8], part), 71), part),
    }


rope_base = 500000.0


def rotate(vectors, positions):
    half = vectors.shape[-1] // 2
    freqs = rope_base ** (-2.0 * jnp.arange(half).astype(jnp.float32) / (2.0 * half))
    angles = positions[:, None] * freqs[None, :]
    cosine = jnp.cos(angles)[:, None, :]
    sine = jnp.sin(angles)[:, None, :]
    first = vectors[..., :half]
    second = vectors[..., half:]
    return jnp.concatenate([first * cosine - second * sine, second * cosine + first * sine], axis=-1)


def attend_row(packed):
    queries_rot, keys_rot, values_b, cache_keys, cache_values, length = packed
    scaling = HD ** -0.5
    scores = jnp.einsum("kgd,kcd->kgc", queries_rot.astype(jnp.float32), cache_keys.astype(jnp.float32)) * scaling
    own_score = jnp.einsum("kgd,kd->kg", queries_rot.astype(jnp.float32), keys_rot.astype(jnp.float32)) * scaling
    valid = jnp.arange(CACHE).astype(jnp.int32) < length
    scores = jnp.where(valid[None, None, :], scores, jnp.float32(-1e30))
    highest = jnp.maximum(jnp.max(scores, axis=-1), own_score)
    weights = jnp.exp(scores - highest[..., None])
    own_weight = jnp.exp(own_score - highest)
    total = jnp.sum(weights, axis=-1) + own_weight
    probs = (weights / total[..., None]).astype(jnp.bfloat16)
    own_prob = (own_weight / total).astype(jnp.bfloat16)
    mixed = jnp.einsum("kgc,kcd->kgd", probs.astype(jnp.float32), cache_values.astype(jnp.float32))
    mixed = mixed + own_prob.astype(jnp.float32)[..., None] * values_b.astype(jnp.float32)[:, None, :]
    return mixed.astype(jnp.bfloat16)


def reference(tokens, w_query, w_key, w_value, w_out, key_cache, value_cache, lengths):
    positions = lengths.astype(jnp.float32)
    queries = jnp.dot(tokens, w_query, preferred_element_type=jnp.float32)
    keys_new = jnp.dot(tokens, w_key, preferred_element_type=jnp.float32)
    values_new = jnp.dot(tokens, w_value, preferred_element_type=jnp.float32)
    queries_rot = rotate(queries.reshape(BATCH, HQ, HD), positions).astype(jnp.bfloat16)
    queries_rot = queries_rot.reshape(BATCH, KVH, HQ // KVH, HD)
    keys_rot = rotate(keys_new.reshape(BATCH, KVH, HD), positions).astype(jnp.bfloat16)
    values_b = values_new.astype(jnp.bfloat16).reshape(BATCH, KVH, HD)
    heads = lax.map(attend_row, (queries_rot, keys_rot, values_b, key_cache, value_cache, lengths))
    heads = heads.reshape(BATCH, HQ * HD)
    return jnp.dot(heads, w_out, preferred_element_type=jnp.float32).astype(jnp.bfloat16)
```

```python
import functools

import jax
import jax.numpy as jnp
from jax import lax
from jax.experimental import pallas as pl
from jax.experimental.pallas import tpu as pltpu
from jax.sharding import PartitionSpec as P

rope_base = 500000.0
f32 = jnp.float32
bf16 = jnp.bfloat16
MESH = pl.DeviceIdType.MESH
LAG = 3


def inner_of(count):
    best = 1
    for size in range(1, count + 1):
        if count % size == 0 and size * size <= count:
            best = size
    return best


def kernel(
    outer, inner, lengths, freqs, tokens, w_query, w_key, w_value, w_out, key_cache, value_cache,
    out, wbuf, wob, kbuf, vbuf, part, got_a, sum_b, got_b, qs, ms, lhs32, lhs, gath, osum, ogot,
    wsem, wosem, csem, a_send, a_recv, b_send, b_recv, z_send, y_send, g_recv, o_send, o_recv,
):
    chunks, _, _, rows, width = part.shape
    count = outer * inner
    kv_cols = w_key.shape[1]
    kv_local, head_dim = kbuf.shape[1], kbuf.shape[3]
    slots = kbuf.shape[2]
    heads_local = qs.shape[1]
    group = heads_local // kv_local
    gcols = group * head_dim
    per_chunk = width // head_dim
    per_group = gcols // width
    me = lax.axis_index("gx")
    core = lax.axis_index("gy")
    o, i = me // inner, me % inner

    def along_z(d):
        return lax.rem(o + d, outer)

    def along_y(d):
        return lax.rem(i + d, inner)

    def q_copy(c):
        cols = pl.ds(pl.multiple_of((c - 1) * width, width), width)
        return pltpu.make_async_copy(w_query.at[:, cols], wbuf.at[c], wsem.at[c])

    k_copy = pltpu.make_async_copy(w_key, wbuf.at[0, :, pl.ds(0, kv_cols)], wsem.at[0])
    v_copy = pltpu.make_async_copy(w_value, wbuf.at[0, :, pl.ds(kv_cols, kv_cols)], wsem.at[chunks])
    kc_copy = pltpu.make_async_copy(key_cache, kbuf, csem.at[0])
    vc_copy = pltpu.make_async_copy(value_cache, vbuf, csem.at[1])
    wo_copies = [
        pltpu.make_async_copy(w_out.at[pl.ds(k * gcols, gcols)], wob.at[k], wosem.at[k])
        for k in range(kv_local)
    ]
    k_copy.start()
    v_copy.start()
    for c in range(1, chunks):
        q_copy(c).start()
    kc_copy.start()
    vc_copy.start()
    for copy in wo_copies:
        copy.start()

    barrier = pltpu.get_barrier_semaphore()
    for d in range(1, outer):
        pl.semaphore_signal(
            barrier, inc=1, device_id={"gx": along_z(d) * inner + i}, device_id_type=MESH
        )
    for d in range(1, inner):
        pl.semaphore_signal(
            barrier, inc=1, device_id={"gx": o * inner + along_y(d)}, device_id_type=MESH
        )
    pl.semaphore_signal(barrier, inc=1, device_id={"gy": 1 - core}, device_id_type=MESH)

    row_ids = lax.broadcasted_iota(jnp.int32, (rows, head_dim), 0)
    positions = jnp.zeros((rows, head_dim), jnp.int32)
    for r in range(rows):
        positions = jnp.where(row_ids == r, lengths[r], positions)
    angles = positions.astype(f32) * freqs[...]
    lanes = lax.broadcasted_iota(jnp.int32, (rows, head_dim), 1)
    cosine = jnp.cos(angles)
    sine = jnp.sin(angles)
    sine = jnp.where(lanes < head_dim // 2, -sine, sine)

    def rotate(x):
        return x * cosine + pltpu.roll(x, head_dim // 2, 1) * sine

    pl.semaphore_wait(barrier, outer - 1 + inner - 1 + 1)

    def a_copy(c, d):
        return pltpu.make_async_remote_copy(
            src_ref=part.at[c, along_y(d)],
            dst_ref=got_a.at[c, i],
            send_sem=a_send.at[c, d],
            recv_sem=a_recv.at[c, i],
            device_id={"gx": o * inner + along_y(d)},
            device_id_type=MESH,
        )

    def a_arrival(c, d):
        src = along_y(d)
        return pltpu.make_async_remote_copy(
            src_ref=got_a.at[c, src],
            dst_ref=got_a.at[c, src],
            send_sem=a_send.at[c, d],
            recv_sem=a_recv.at[c, src],
            device_id={"gx": o * inner + src},
            device_id_type=MESH,
        )

    def b_copy(c, d):
        return pltpu.make_async_remote_copy(
            src_ref=sum_b.at[c, along_z(d)],
            dst_ref=got_b.at[c, o],
            send_sem=b_send.at[c, d],
            recv_sem=b_recv.at[c, o],
            device_id={"gx": along_z(d) * inner + i},
            device_id_type=MESH,
        )

    def b_arrival(c, d):
        src = along_z(d)
        return pltpu.make_async_remote_copy(
            src_ref=got_b.at[c, src],
            dst_ref=got_b.at[c, src],
            send_sem=b_send.at[c, d],
            recv_sem=b_recv.at[c, src],
            device_id={"gx": src * inner + i},
            device_id_type=MESH,
        )

    def second_stage(c):
        total = part[c, i]
        for d in range(1, inner):
            a_arrival(c, d).wait_recv()
            total = total + got_a[c, along_y(d)]
        sum_b[c] = total
        for d in range(1, outer):
            b_copy(c, d).start()

    k_copy.wait()
    v_copy.wait()

    def project(c, carry):
        @pl.when(c > 0)
        def _():
            q_copy(c).wait()

        acc = jnp.dot(tokens[...], wbuf[c], preferred_element_type=f32)
        for p in range(count):
            part[c, p % inner, p // inner] = acc[p * rows : (p + 1) * rows, :]
        for d in range(1, inner):
            a_copy(c, d).start()

        @pl.when(c >= LAG)
        def _():
            second_stage(c - LAG)

        return carry

    lax.fori_loop(0, chunks, project, 0)
    for c in range(max(chunks - LAG, 0), chunks):
        second_stage(c)

    def reduced(c):
        total = sum_b[c, o]
        for d in range(1, outer):
            b_arrival(c, d).wait_recv()
            total = total + got_b[c, along_z(d)]
        return total

    key_values = reduced(0)
    keys_rot = [
        rotate(key_values[:, k * head_dim : (k + 1) * head_dim]).astype(bf16).astype(f32)
        for k in range(kv_local)
    ]
    values_b = [
        key_values[:, kv_cols + k * head_dim : kv_cols + (k + 1) * head_dim].astype(bf16).astype(f32)
        for k in range(kv_local)
    ]
    kc_copy.wait()
    vc_copy.wait()
    scaling = head_dim ** (-0.5)
    slot_ids = lax.broadcasted_iota(jnp.int32, (group, slots), 1)

    def g_copy(k, src_o, sem, target):
        return pltpu.make_async_remote_copy(
            src_ref=gath.at[k, i, src_o],
            dst_ref=gath.at[k, i, src_o],
            send_sem=sem,
            recv_sem=g_recv.at[k, i, src_o],
            device_id={"gx": target},
            device_id_type=MESH,
        )

    def g_arrival(k, src_i, src_o):
        return pltpu.make_async_remote_copy(
            src_ref=gath.at[k, src_i, src_o],
            dst_ref=gath.at[k, src_i, src_o],
            send_sem=z_send.at[k, 0],
            recv_sem=g_recv.at[k, src_i, src_o],
            device_id={"gx": lax.rem(me + 1, count)},
            device_id_type=MESH,
        )

    def forward(k, d):
        src = along_z(d)
        if d > 0:
            g_arrival(k, i, src).wait_recv()
        for e in range(1, inner):
            g_copy(k, src, y_send.at[k, d, e], o * inner + along_y(e)).start()

    for k in range(kv_local):
        for c in range(1 + k * per_group, 1 + (k + 1) * per_group):
            chunk = reduced(c)
            for h in range(per_chunk):
                qs[:, (c - 1) * per_chunk + h, :] = rotate(
                    chunk[:, h * head_dim : (h + 1) * head_dim]
                )
        for r in range(rows):
            query = qs[r, k * group : (k + 1) * group, :].astype(bf16)
            scores = (
                lax.dot_general(
                    query, kbuf[r, k], (((1,), (1,)), ((), ())), preferred_element_type=f32
                )
                * scaling
            )
            own = (
                jnp.sum(query.astype(f32) * keys_rot[k][r : r + 1, :], axis=-1, keepdims=True)
                * scaling
            )
            scores = jnp.where(slot_ids < lengths[r], scores, f32(-1e30))
            highest = jnp.maximum(jnp.max(scores, axis=-1, keepdims=True), own)
            weights = jnp.exp(scores - highest)
            own_weight = jnp.exp(own - highest)
            total = jnp.sum(weights, axis=-1, keepdims=True) + own_weight
            scale = 1.0 / total
            probs = (weights * scale).astype(bf16)
            own_prob = (own_weight * scale).astype(bf16).astype(f32)
            mixed = jnp.dot(probs, vbuf[r, k], preferred_element_type=f32)
            ms[r, k * group : (k + 1) * group, :] = mixed + own_prob * values_b[k][r : r + 1, :]
        for h in range(group):
            gath[k, i, o, :, h * head_dim : (h + 1) * head_dim] = ms[:, k * group + h, :].astype(
                bf16
            )
        for d in range(1, outer):
            g_copy(k, o, z_send.at[k, d], along_z(d) * inner + i).start()
        forward(k, 0)

    for k in range(kv_local):
        for d in range(1, outer):
            forward(k, d)

    tiles, _, half, tile = osum.shape

    def o_copy(j):
        return pltpu.make_async_remote_copy(
            src_ref=osum.at[j, 1 - core],
            dst_ref=ogot.at[j],
            send_sem=o_send.at[j],
            recv_sem=o_recv.at[j],
            device_id={"gy": 1 - core},
            device_id_type=MESH,
        )

    for k in range(kv_local):
        for e in range(1, inner):
            for d in range(outer):
                g_arrival(k, along_y(e), along_z(d)).wait_recv()
        for p in range(count):
            lhs32[p * rows : (p + 1) * rows, :] = gath[k, p % inner, p // inner].astype(f32)
        lhs[k] = lhs32[...].astype(bf16)
        wo_copies[k].wait()

        def multiply(j, carry):
            cols = pl.ds(pl.multiple_of(j * tile, tile), tile)
            term = jnp.dot(lhs[k], wob[k, :, cols], preferred_element_type=f32)
            if k > 0:
                term = term + osum[j].reshape(2 * half, tile)
            osum[j] = term.reshape(2, half, tile)
            if k == kv_local - 1:
                o_copy(j).start()
            return carry

        lax.fori_loop(0, tiles, multiply, 0)

    for j in range(tiles):
        o_copy(j).wait()
        out[:, j * tile : (j + 1) * tile] = (osum[j, core] + ogot[j]).astype(out.dtype)

    def drain(c, carry):
        for d in range(1, inner):
            a_copy(c, d).wait_send()
        for d in range(1, outer):
            b_copy(c, d).wait_send()
        return carry

    lax.fori_loop(0, chunks, drain, 0)
    for k in range(kv_local):
        for d in range(1, outer):
            g_copy(k, o, z_send.at[k, d], along_z(d) * inner + i).wait_send()
        for d in range(outer):
            for e in range(1, inner):
                g_copy(k, along_z(d), y_send.at[k, d, e], o * inner + along_y(e)).wait_send()


def on_device(count, tokens, w_query, w_key, w_value, w_out, key_cache, value_cache, lengths):
    rows, kv_local, slots, head_dim = key_cache.shape
    inner = inner_of(count)
    outer = count // inner
    batch, depth = tokens.shape
    query_cols = w_query.shape[1]
    width = 2 * w_key.shape[1]
    chunks = 1 + query_cols // width
    heads_local = query_cols // head_dim
    gcols = query_cols // kv_local
    out_cols = w_out.shape[1]
    tile = min(256, out_cols)
    tiles = out_cols // tile
    freqs = rope_base ** (-2.0 * jnp.arange(head_dim // 2).astype(f32) / head_dim)
    freqs = jnp.concatenate([freqs, freqs])[None, :]
    any_spec = pl.BlockSpec(memory_space=pl.ANY)
    vmem = pl.BlockSpec(memory_space=pltpu.VMEM)
    smem = pl.BlockSpec(memory_space=pltpu.SMEM)
    dma = pltpu.SemaphoreType.DMA
    return pl.pallas_call(
        functools.partial(kernel, outer, inner),
        out_shape=jax.ShapeDtypeStruct((batch // 2, out_cols), bf16),
        in_specs=[smem, vmem, vmem] + [any_spec] * 6,
        out_specs=vmem,
        scratch_shapes=[
            pltpu.VMEM((chunks, depth, width), bf16),
            pltpu.VMEM((kv_local, gcols, out_cols), bf16),
            pltpu.VMEM(key_cache.shape, bf16),
            pltpu.VMEM(value_cache.shape, bf16),
            pltpu.VMEM((chunks, inner, outer, rows, width), f32),
            pltpu.VMEM((chunks, inner, outer, rows, width), f32),
            pltpu.VMEM((chunks, outer, rows, width), f32),
            pltpu.VMEM((chunks, outer, rows, width), f32),
            pltpu.VMEM((rows, heads_local, head_dim), f32),
            pltpu.VMEM((rows, heads_local, head_dim), f32),
            pltpu.VMEM((batch, gcols), f32),
            pltpu.VMEM((kv_local, batch, gcols), bf16),
            pltpu.VMEM((kv_local, inner, outer, rows, gcols), bf16),
            pltpu.VMEM((tiles, 2, batch // 2, tile), f32),
            pltpu.VMEM((tiles, batch // 2, tile), f32),
            dma((chunks + 1,)),
            dma((kv_local,)),
            dma((2,)),
            dma((chunks, inner)),
            dma((chunks, inner)),
            dma((chunks, outer)),
            dma((chunks, outer)),
            dma((kv_local, outer)),
            dma((kv_local, outer, inner)),
            dma((kv_local, inner, outer)),
            dma((tiles,)),
            dma((tiles,)),
        ],
        compiler_params=pltpu.CompilerParams(
            collective_id=0, has_side_effects=True, vmem_limit_bytes=60 * 2**20
        ),
        name="decode_attention",
    )(lengths, freqs, tokens, w_query, w_key, w_value, w_out, key_cache, value_cache)


def solution(mesh):
    in_specs = (
        P("groups", "gx"),
        P("gx", "gy"),
        P("gx", "gy"),
        P("gx", "gy"),
        P("gy", "gx"),
        P(("groups", "gx"), "gy", None, None),
        P(("groups", "gx"), "gy", None, None),
        P(("groups", "gx")),
    )
    out_specs = P(("groups", "gy"), "gx")
    return jax.shard_map(
        functools.partial(on_device, mesh.shape["gx"]),
        mesh=mesh,
        in_specs=in_specs,
        out_specs=out_specs,
        check_vma=False,
    )
```

```python
import functools
import math

import jax
import jax.numpy as jnp
from jax import lax
from jax.experimental import pallas as pl
from jax.experimental.pallas import tpu as pltpu
from jax.sharding import PartitionSpec as P

rope_base = 500000.0
f32 = jnp.float32
bf16 = jnp.bfloat16
MESH = pl.DeviceIdType.MESH
LAG = 5
DEPTH = 6
GREET = 0
DIRECT = 8


def inner_of(count):
    best = 1
    for size in range(1, count + 1):
        if count % size == 0 and size * size <= count:
            best = size
    return best


def kernel(
    outer, inner, lengths, tokens, w_query, w_key, w_value, w_out, key_cache, value_cache,
    out, tbuf, wbuf, wob, kbuf, vbuf, part, got_a, sum_b, got_b, qs, ms, lhs32, lhs, gath, osum, ogot,
    wsem, wosem, csem, a_send, a_recv, b_send, b_recv, z_send, y_send, g_recv, o_send, o_recv,
):
    chunks, _, _, rows, width = part.shape
    count = outer * inner
    kv_cols = w_key.shape[1]
    kv_local, head_dim = kbuf.shape[1], kbuf.shape[3]
    slots = kbuf.shape[2]
    heads_local = qs.shape[1]
    group = heads_local // kv_local
    gcols = group * head_dim
    per_chunk = width // head_dim
    per_group = gcols // width
    me = lax.axis_index("gx")
    core = lax.axis_index("gy")
    o, i = me // inner, me % inner

    def along_z(d):
        return lax.rem(o + d, outer)

    def along_y(d):
        return lax.rem(i + d, inner)

    def q_copy(c):
        cols = pl.ds(pl.multiple_of((c - 1) * width, width), width)
        return pltpu.make_async_copy(w_query.at[:, cols], wbuf.at[c], wsem.at[c])

    k_copy = pltpu.make_async_copy(w_key, wbuf.at[0, :, pl.ds(0, kv_cols)], wsem.at[0])
    v_copy = pltpu.make_async_copy(w_value, wbuf.at[0, :, pl.ds(kv_cols, kv_cols)], wsem.at[chunks])
    kc_copy = pltpu.make_async_copy(key_cache, kbuf, csem.at[0])
    vc_copy = pltpu.make_async_copy(value_cache, vbuf, csem.at[1])
    pieces = wosem.shape[1]
    piece = gcols // pieces

    def wo_copy(k, t):
        return pltpu.make_async_copy(
            w_out.at[pl.ds(k * gcols + t * piece, piece)],
            wob.at[k, pl.ds(t * piece, piece)],
            wosem.at[k, t],
        )

    later = [kc_copy, vc_copy] + [wo_copy(k, t) for k in range(kv_local) for t in range(pieces)]
    t_copy = pltpu.make_async_copy(tokens, tbuf, csem.at[2])
    t_copy.start()
    k_copy.start()
    v_copy.start()
    for c in range(1, min(DEPTH, chunks)):
        q_copy(c).start()

    barrier = pltpu.get_barrier_semaphore()
    direct = count <= DIRECT
    if direct:
        for d in range(1, count):
            pl.semaphore_signal(
                barrier, inc=1, device_id={"gx": lax.rem(me + d, count)}, device_id_type=MESH
            )
    else:
        for d in range(1, outer):
            pl.semaphore_signal(
                barrier, inc=1, device_id={"gx": along_z(d) * inner + i}, device_id_type=MESH
            )
        for d in range(1, inner):
            pl.semaphore_signal(
                barrier, inc=1, device_id={"gx": o * inner + along_y(d)}, device_id_type=MESH
            )
    pl.semaphore_signal(barrier, inc=1, device_id={"gy": 1 - core}, device_id_type=MESH)

    row_ids = lax.broadcasted_iota(jnp.int32, (rows, head_dim), 0)
    positions = jnp.zeros((rows, head_dim), jnp.int32)
    for r in range(rows):
        positions = jnp.where(row_ids == r, lengths[r], positions)
    lanes = lax.broadcasted_iota(jnp.int32, (rows, head_dim), 1)
    index = lax.rem(lanes, head_dim // 2).astype(f32)
    angles = positions.astype(f32) * jnp.exp(index * (-2.0 / head_dim * math.log(rope_base)))
    cosine = jnp.cos(angles)
    sine = jnp.sin(angles)
    sine = jnp.where(lanes < head_dim // 2, -sine, sine)

    def rotate(x):
        return x * cosine + pltpu.roll(x, head_dim // 2, 1) * sine

    greeted = count if direct else outer + inner - 1
    greet_at = min(GREET, chunks - 1)

    def a_copy(c, d):
        return pltpu.make_async_remote_copy(
            src_ref=part.at[c, along_y(d)],
            dst_ref=got_a.at[c, i],
            send_sem=a_send.at[c, d],
            recv_sem=a_recv.at[c, i],
            device_id={"gx": o * inner + along_y(d)},
            device_id_type=MESH,
        )

    def a_arrival(c, d):
        src = along_y(d)
        return pltpu.make_async_remote_copy(
            src_ref=got_a.at[c, src],
            dst_ref=got_a.at[c, src],
            send_sem=a_send.at[c, d],
            recv_sem=a_recv.at[c, src],
            device_id={"gx": o * inner + src},
            device_id_type=MESH,
        )

    def b_copy(c, d):
        return pltpu.make_async_remote_copy(
            src_ref=sum_b.at[c, along_z(d)],
            dst_ref=got_b.at[c, o],
            send_sem=b_send.at[c, d],
            recv_sem=b_recv.at[c, o],
            device_id={"gx": along_z(d) * inner + i},
            device_id_type=MESH,
        )

    def b_arrival(c, d):
        src = along_z(d)
        return pltpu.make_async_remote_copy(
            src_ref=got_b.at[c, src],
            dst_ref=got_b.at[c, src],
            send_sem=b_send.at[c, d],
            recv_sem=b_recv.at[c, src],
            device_id={"gx": src * inner + i},
            device_id_type=MESH,
        )

    def second_stage(c):
        total = part[c, i]
        for d in range(1, inner):
            a_arrival(c, d).wait_recv()
            total = total + got_a[c, along_y(d)]
        sum_b[c] = total
        for d in range(1, outer):
            b_copy(c, d).start()

    t_copy.wait()
    k_copy.wait()
    v_copy.wait()

    def project(c, carry):
        @pl.when(c > 0)
        def _():
            q_copy(c).wait()

        @pl.when(c + DEPTH < chunks)
        def _():
            q_copy(c + DEPTH).start()

        for t, copy in enumerate(later[:DEPTH]):

            @pl.when(c + DEPTH == chunks + t)
            def _():
                copy.start()

        acc = jnp.dot(tbuf[...], wbuf[c], preferred_element_type=f32)
        for p in range(count):
            part[c, p % inner, p // inner] = acc[p * rows : (p + 1) * rows, :]
        @pl.when(c == greet_at)
        def _():
            pl.semaphore_wait(barrier, greeted)
            for early in range(greet_at):
                for d in range(1, inner):
                    a_copy(early, d).start()

        @pl.when(c >= greet_at)
        def _():
            for d in range(1, inner):
                a_copy(c, d).start()

        @pl.when(c >= LAG)
        def _():
            second_stage(c - LAG)

        return carry

    lax.fori_loop(0, chunks, project, 0)
    for copy in later[DEPTH:]:
        copy.start()
    for c in range(max(chunks - LAG, 0), chunks):
        second_stage(c)

    def reduced(c):
        total = sum_b[c, o]
        for d in range(1, outer):
            b_arrival(c, d).wait_recv()
            total = total + got_b[c, along_z(d)]
        return total

    key_values = reduced(0)
    keys_rot = [
        rotate(key_values[:, k * head_dim : (k + 1) * head_dim]).astype(bf16).astype(f32)
        for k in range(kv_local)
    ]
    values_b = [
        key_values[:, kv_cols + k * head_dim : kv_cols + (k + 1) * head_dim].astype(bf16).astype(f32)
        for k in range(kv_local)
    ]
    kc_copy.wait()
    vc_copy.wait()
    scaling = head_dim ** (-0.5)
    slot_ids = lax.broadcasted_iota(jnp.int32, (group, slots), 1)

    def g_copy(k, src_o, sem, target):
        return pltpu.make_async_remote_copy(
            src_ref=gath.at[k, i, src_o],
            dst_ref=gath.at[k, i, src_o],
            send_sem=sem,
            recv_sem=g_recv.at[k, i, src_o],
            device_id={"gx": target},
            device_id_type=MESH,
        )

    def g_arrival(k, src_i, src_o):
        return pltpu.make_async_remote_copy(
            src_ref=gath.at[k, src_i, src_o],
            dst_ref=gath.at[k, src_i, src_o],
            send_sem=z_send.at[k, 0],
            recv_sem=g_recv.at[k, src_i, src_o],
            device_id={"gx": lax.rem(me + 1, count)},
            device_id_type=MESH,
        )

    def forward(k, d):
        src = along_z(d)
        if d > 0:
            g_arrival(k, i, src).wait_recv()
        for e in range(1, inner):
            g_copy(k, src, y_send.at[k, d, e], o * inner + along_y(e)).start()

    for k in range(kv_local):
        for c in range(1 + k * per_group, 1 + (k + 1) * per_group):
            chunk = reduced(c)
            for h in range(per_chunk):
                qs[:, (c - 1) * per_chunk + h, :] = rotate(
                    chunk[:, h * head_dim : (h + 1) * head_dim]
                )
        for r in range(rows):
            query = qs[r, k * group : (k + 1) * group, :].astype(bf16)
            scores = (
                lax.dot_general(
                    query, kbuf[r, k], (((1,), (1,)), ((), ())), preferred_element_type=f32
                )
                * scaling
            )
            own = (
                jnp.sum(query.astype(f32) * keys_rot[k][r : r + 1, :], axis=-1, keepdims=True)
                * scaling
            )
            scores = jnp.where(slot_ids < lengths[r], scores, f32(-1e30))
            highest = jnp.maximum(jnp.max(scores, axis=-1, keepdims=True), own)
            weights = jnp.exp(scores - highest)
            own_weight = jnp.exp(own - highest)
            total = jnp.sum(weights, axis=-1, keepdims=True) + own_weight
            scale = 1.0 / total
            probs = (weights * scale).astype(bf16)
            own_prob = (own_weight * scale).astype(bf16).astype(f32)
            mixed = jnp.dot(probs, vbuf[r, k], preferred_element_type=f32)
            ms[r, k * group : (k + 1) * group, :] = mixed + own_prob * values_b[k][r : r + 1, :]
        for h in range(group):
            gath[k, i, o, :, h * head_dim : (h + 1) * head_dim] = ms[:, k * group + h, :].astype(
                bf16
            )
        if direct:
            for d in range(1, outer):
                for e in range(inner):
                    g_copy(k, o, y_send.at[k, d, e], along_z(d) * inner + along_y(e)).start()
            for e in range(1, inner):
                g_copy(k, o, y_send.at[k, 0, e], o * inner + along_y(e)).start()
        else:
            for d in range(1, outer):
                g_copy(k, o, z_send.at[k, d], along_z(d) * inner + i).start()
            forward(k, 0)

    for k in range(0 if direct else kv_local):
        for d in range(1, outer):
            forward(k, d)

    tiles, _, half, tile = osum.shape

    def o_copy(j):
        return pltpu.make_async_remote_copy(
            src_ref=osum.at[j, 1 - core],
            dst_ref=ogot.at[j],
            send_sem=o_send.at[j],
            recv_sem=o_recv.at[j],
            device_id={"gy": 1 - core},
            device_id_type=MESH,
        )

    for k in range(kv_local):
        for e in range(inner):
            for d in range(outer):
                if e > 0 or (direct and d > 0):
                    g_arrival(k, along_y(e), along_z(d)).wait_recv()
        for p in range(count):
            lhs32[p * rows : (p + 1) * rows, :] = gath[k, p % inner, p // inner].astype(f32)
        lhs[k] = lhs32[...].astype(bf16)
        for t in range(pieces):
            wo_copy(k, t).wait()

        def multiply(j, carry):
            cols = pl.ds(pl.multiple_of(j * tile, tile), tile)
            term = jnp.dot(lhs[k], wob[k, :, cols], preferred_element_type=f32)
            if k > 0:
                term = term + osum[j].reshape(2 * half, tile)
            osum[j] = term.reshape(2, half, tile)
            if k == kv_local - 1:
                o_copy(j).start()
            return carry

        lax.fori_loop(0, tiles, multiply, 0)

    for j in range(tiles):
        o_copy(j).wait()
        out[:, j * tile : (j + 1) * tile] = (osum[j, core] + ogot[j]).astype(out.dtype)

    def drain(c, carry):
        for d in range(1, inner):
            a_copy(c, d).wait_send()
        for d in range(1, outer):
            b_copy(c, d).wait_send()
        return carry

    lax.fori_loop(0, chunks, drain, 0)
    for k in range(kv_local):
        if not direct:
            for d in range(1, outer):
                g_copy(k, o, z_send.at[k, d], along_z(d) * inner + i).wait_send()
        for d in range(outer):
            for e in range(0 if direct and d > 0 else 1, inner):
                g_copy(k, along_z(d), y_send.at[k, d, e], o * inner + along_y(e)).wait_send()


def on_device(count, tokens, w_query, w_key, w_value, w_out, key_cache, value_cache, lengths):
    rows, kv_local, slots, head_dim = key_cache.shape
    inner = inner_of(count)
    outer = count // inner
    batch, depth = tokens.shape
    query_cols = w_query.shape[1]
    width = 2 * w_key.shape[1]
    chunks = 1 + query_cols // width
    heads_local = query_cols // head_dim
    gcols = query_cols // kv_local
    out_cols = w_out.shape[1]
    tile = min(256, out_cols)
    tiles = out_cols // tile
    any_spec = pl.BlockSpec(memory_space=pl.ANY)
    vmem = pl.BlockSpec(memory_space=pltpu.VMEM)
    smem = pl.BlockSpec(memory_space=pltpu.SMEM)
    dma = pltpu.SemaphoreType.DMA
    return pl.pallas_call(
        functools.partial(kernel, outer, inner),
        out_shape=jax.ShapeDtypeStruct((batch // 2, out_cols), bf16),
        in_specs=[smem] + [any_spec] * 7,
        out_specs=vmem,
        scratch_shapes=[
            pltpu.VMEM(tokens.shape, bf16),
            pltpu.VMEM((chunks, depth, width), bf16),
            pltpu.VMEM((kv_local, gcols, out_cols), bf16),
            pltpu.VMEM(key_cache.shape, bf16),
            pltpu.VMEM(value_cache.shape, bf16),
            pltpu.VMEM((chunks, inner, outer, rows, width), f32),
            pltpu.VMEM((chunks, inner, outer, rows, width), f32),
            pltpu.VMEM((chunks, outer, rows, width), f32),
            pltpu.VMEM((chunks, outer, rows, width), f32),
            pltpu.VMEM((rows, heads_local, head_dim), f32),
            pltpu.VMEM((rows, heads_local, head_dim), f32),
            pltpu.VMEM((batch, gcols), f32),
            pltpu.VMEM((kv_local, batch, gcols), bf16),
            pltpu.VMEM((kv_local, inner, outer, rows, gcols), bf16),
            pltpu.VMEM((tiles, 2, batch // 2, tile), f32),
            pltpu.VMEM((tiles, batch // 2, tile), f32),
            dma((chunks + 1,)),
            dma((kv_local, 4)),
            dma((3,)),
            dma((chunks, inner)),
            dma((chunks, inner)),
            dma((chunks, outer)),
            dma((chunks, outer)),
            dma((kv_local, outer)),
            dma((kv_local, outer, inner)),
            dma((kv_local, inner, outer)),
            dma((tiles,)),
            dma((tiles,)),
        ],
        compiler_params=pltpu.CompilerParams(
            collective_id=0, has_side_effects=True, vmem_limit_bytes=60 * 2**20
        ),
        name="decode_attention",
    )(lengths, tokens, w_query, w_key, w_value, w_out, key_cache, value_cache)


def solution(mesh):
    in_specs = (
        P("groups", "gx"),
        P("gx", "gy"),
        P("gx", "gy"),
        P("gx", "gy"),
        P("gy", "gx"),
        P(("groups", "gx"), "gy", None, None),
        P(("groups", "gx"), "gy", None, None),
        P(("groups", "gx")),
    )
    out_specs = P(("groups", "gy"), "gx")
    return jax.shard_map(
        functools.partial(on_device, mesh.shape["gx"]),
        mesh=mesh,
        in_specs=in_specs,
        out_specs=out_specs,
        check_vma=False,
    )
```
